256 devices in a mesh: row: 8 (over z), col: 32 (over x, y, core).
Axes of the slice: x: 4, y: 4, z: 8, core: 2. Of those that a mesh axis runs over, the one named last changes fastest.
Arguments:
- rhs_super: bfloat16 [2, 2, 8, 128, 512], P(None, None, 'row'), may hold values from -6 to 6
- factor_super: bfloat16 [2, 2, 8, 128, 1, 32, 128], P(None, None, 'row', None, None, 'col'), may hold values from -0.125 to 0.125
- mask_super: int32 [2, 2, 8, 1, 32], P(None, None, 'row', None, 'col'), may hold values 0 or 1
- dinv_rows: bfloat16 [1, 32, 128, 2048], P(None, 'col'), may hold values from -0.125 to 0.125
- factor_trail: bfloat16 [32, 8, 128, 1, 32, 128], P(None, 'row', None, None, 'col'), may hold values from -0.125 to 0.125
- mask_trail: int32 [32, 8, 1, 32], P(None, 'row', None, 'col'), may hold values 0 or 1
- rhs_trail: bfloat16 [32, 1, 8, 128, 512], P('col', None, 'row'), may hold values from -6 to 6
Outputs:
- solved: bfloat16 [1, 32, 128, 512], P(None, 'col')
- remaining: bfloat16 [32, 1, 8, 128, 512], P('col', None, 'row')
The draws below stay inside these ranges and needn't reach their ends.
All inputs are finite; a program needn't handle non-finite values. No bound on the sum of `mask_super` or of `mask_trail` on one device may be relied on, other than what follows from the above.
Results may differ from the reference program's by a relative error of at most 0.0048.
Values may be sent and summed in bfloat16 or wider, within the bound.
No kernel may reach another device: no remote copies, remote signals or barrier semaphores. Data moves between devices by JAX's collectives and lax.ppermute only.
A program may use at most 64 MiB of HBM per device.

```python
import jax
import jax.numpy as jnp

TB = 128
ST = 16
NSB = 2
K = 512
TQ = 1
SB = 2048
NS = 4096
SQ = 2
JT_DEV = 1
ITR = 32
N_ROW = 8
N_COL = 32


def touch_ends(entries, stream_key, least, high):
    longest = entries.shape.index(max(entries.shape))
    spots = []
    for shift in (0, 1):
        where = [jax.random.randint(jax.random.fold_in(stream_key, axis), (), 0, length) for axis, length in enumerate(entries.shape)]
        where[longest] = (where[longest] + shift) % entries.shape[longest]
        spots.append(tuple(where))
    return entries.at[spots[0]].set(least).at[spots[1]].set(high)


def levels(stream_key, extent, split, smallest, largest):
    loudness, own = 1.0, jax.random.fold_in(stream_key, 6)
    for axis_at, shards_of in split:
        draws = jnp.exp(jax.random.uniform(jax.random.fold_in(own, axis_at), (shards_of,), jnp.float32, smallest / len(split), largest / len(split)))
        loudness = loudness * jnp.repeat(draws, extent[axis_at] // shards_of).reshape([-1 if axis == axis_at else 1 for axis in range(len(extent))])
    return loudness


def gaussian(own_key, extent, spread, bound, split=(), held_as=jnp.bfloat16):
    gain = levels(own_key, extent, split, -0.22, 0.18) if split else 1.0
    values = jax.random.normal(own_key, extent, jnp.float32) * spread * gain
    return jnp.minimum(jnp.maximum(values, -bound), bound).astype(held_as)


def setup_inputs(seed: int = 0) -> dict:
    keys = jax.random.split(jax.random.key(seed), 8)
    return {
        "rhs_super": gaussian(keys[0], (NSB, SQ, N_ROW, TB, K), 1.0, 6.0, ((2, 8),)),
        "factor_super": gaussian(keys[1], (NSB, SQ, N_ROW, TB, JT_DEV, N_COL, TB), SB ** -0.5, 0.125, ((2, 8), (5, 32))),
        "mask_super": touch_ends((jax.random.randint(keys[2], (NSB, SQ, N_ROW, JT_DEV, N_COL), 0, 2) < 1).astype(jnp.int32), jax.random.fold_in(keys[2], 1), 0, 1),
        "dinv_rows": gaussian(keys[3], (JT_DEV, N_COL, TB, SB), SB ** -0.5, 0.125, ((1, 32),)),
        "factor_trail": gaussian(keys[4], (ITR, N_ROW, TB, JT_DEV, N_COL, TB), (NS // 2) ** -0.5, 0.125, ((1, 8), (4, 32))),
        "mask_trail": touch_ends((jax.random.randint(keys[5], (ITR, N_ROW, JT_DEV, N_COL), 0, 2) < 1).astype(jnp.int32), jax.random.fold_in(keys[5], 1), 0, 1),
        "rhs_trail": gaussian(keys[6], (N_COL, TQ, N_ROW, TB, K), 1.0, 6.0, ((0, 32), (2, 8))),
    }


def reference(rhs_super, factor_super, mask_super, dinv_rows, factor_trail, mask_trail, rhs_trail):
    tile_count = NSB * ST
    solved_count = tile_count * TB
    block_rows = ST * TB
    owners = jnp.arange(tile_count, dtype=jnp.int32) // ST
    earlier = (owners[:, None] > owners[None, :]).astype(jnp.int32)
    keep_super = (mask_super.reshape(tile_count, tile_count) * earlier).astype(jnp.bfloat16)
    lower_tiles = factor_super.reshape(tile_count, TB, tile_count, TB) * keep_super[:, None, :, None]
    lower_tiles = lower_tiles.reshape(solved_count, solved_count)
    inverse = dinv_rows.reshape(NSB, block_rows, block_rows)
    given_rows = rhs_super.reshape(NSB, block_rows, K)
    solved = jnp.zeros((solved_count, K), jnp.bfloat16)
    for block in range(NSB):
        reached = jnp.dot(lower_tiles[block * block_rows:(block + 1) * block_rows], solved, preferred_element_type=jnp.float32)
        due_rows = (given_rows[block].astype(jnp.float32) - reached).astype(jnp.bfloat16)
        freshly = jnp.dot(inverse[block], due_rows, preferred_element_type=jnp.float32).astype(jnp.bfloat16)
        solved = solved.at[block * block_rows:(block + 1) * block_rows].set(freshly)
    keep_trail = mask_trail.astype(jnp.bfloat16)[:, :, None, :, :, None]
    trail_tiles = (factor_trail * keep_trail).reshape(-1, solved_count)
    reached = jnp.dot(trail_tiles, solved, preferred_element_type=jnp.float32)
    remaining = (rhs_trail.reshape(-1, K).astype(jnp.float32) - reached).astype(jnp.bfloat16)
    return solved.reshape(dinv_rows.shape[0], dinv_rows.shape[1], TB, K), remaining.reshape(rhs_trail.shape)
```

```python
import jax
import jax.numpy as jnp
from jax import lax
from jax.sharding import Mesh
from jax.sharding import PartitionSpec as P

TB = 128
COL = ("x", "y", "core")
CHIP = ("x", "y")
ROWS = 8
CHIPS = 16
KH = 256
F32 = jnp.float32
BF16 = jnp.bfloat16


def exchange(x, axis):
    return lax.all_to_all(x, axis, split_axis=0, concat_axis=0, tiled=True)


def copies(x, axis, n):
    return exchange(jnp.broadcast_to(x, (n, *x.shape)), axis)


def partner(x):
    return lax.ppermute(x, "core", [(0, 1), (1, 0)])


def across(x):
    return lax.ppermute(x, CHIP, [(i, (i + 8) % CHIPS) for i in range(CHIPS)])


def dot_nt(a, b):
    return lax.dot_general(a, b, (((1,), (1,)), ((), ())), preferred_element_type=F32)


def natural(x, core):
    return jnp.where(core == 0, x, jnp.roll(x, TB, axis=1))


def body(rhs_super, factor_super, mask_super, dinv_rows, factor_trail, mask_trail, rhs_trail):
    core = lax.axis_index("core")
    chip = lax.axis_index(CHIP)
    dinv = dinv_rows[0, 0]

    rhs0 = rhs_super[0, :, 0].reshape(2 * TB, 512)
    rhs0_t = lax.dynamic_slice(rhs0, (0, core * KH), (2 * TB, KH)).T
    due0 = exchange(rhs0_t.reshape(ROWS, 32, 2 * TB), "row")
    due0 = due0.reshape(ROWS, 32, 2, TB).transpose(1, 2, 0, 3).reshape(32, 2048)
    dinv_other = partner(dinv)
    solved0 = jnp.concatenate([dot_nt(due0, dinv), dot_nt(due0, dinv_other)], 1).astype(BF16)
    solved0 = copies(solved0, "row", ROWS).reshape(KH, 2 * TB)

    keep = mask_super[1].astype(BF16).reshape(2, 1, 1)
    tiles10 = (factor_super[1].reshape(2, TB, TB) * keep).reshape(2 * TB, TB)
    tiles10 = jnp.concatenate([tiles10, partner(tiles10)], 1)
    reached = dot_nt(solved0, tiles10)
    reached = exchange(reached.reshape(CHIPS, 16, 2 * TB), CHIP)[:8].sum(0)
    rhs1 = rhs_super[1, :, 0].reshape(2 * TB, 512)
    rhs1_t = lax.dynamic_slice(rhs1, (0, core * KH + chip * 16), (2 * TB, 16)).T
    due1 = (rhs1_t.astype(F32) - reached).astype(BF16)

    row = lax.axis_index("row")
    d1 = lax.dynamic_index_in_dim(dinv.reshape(TB, 2, ROWS, TB), row, 2, False).reshape(TB, 2 * TB)
    d1_low = across(d1[TB // 2 :])
    d1_sent = jnp.where(chip >= 8, d1[: TB // 2], d1_low)
    d1_all = copies(d1_sent, CHIP, CHIPS)
    d1_own = jnp.concatenate([d1_all[8:], d1_all[:8]], 1).reshape(8 * TB, 2 * TB)
    d1_other = partner(d1_own)
    part = jnp.concatenate(
        [dot_nt(due1, d1_own).reshape(16, 8, TB), dot_nt(due1, d1_other).reshape(16, 8, TB)], 2
    ).transpose(1, 0, 2)
    solved1 = exchange(part, "row").sum(0).astype(BF16)
    solved1 = copies(natural(solved1, core), "row", ROWS)
    solved1 = solved1.transpose(1, 0, 2).reshape(16, 2048)
    solved1 = copies(solved1, CHIP, CHIPS).reshape(KH, 2048)

    keep_trail = mask_trail.astype(BF16).reshape(32, 1, 1)
    tiles = exchange(factor_trail.reshape(32, TB, TB) * keep_trail, COL)
    tiles0 = tiles[:16].reshape(8, 2, TB, TB).transpose(2, 1, 0, 3).reshape(TB, 2048)
    tiles1 = tiles[16:].transpose(1, 0, 2).reshape(TB, 2048)
    tiles0 = jnp.concatenate([tiles0, partner(tiles0)], 0)
    tiles1 = jnp.concatenate([tiles1, partner(tiles1)], 0)
    solved0 = natural(solved0, core)
    sent0 = jnp.where(chip < 8, solved0[:, :TB], across(solved0[:, TB:]))
    all0 = copies(sent0, CHIP, CHIPS).transpose(1, 0, 2).reshape(KH, 2048)
    total = dot_nt(tiles0, all0) + dot_nt(tiles1, solved1)
    given = rhs_trail.reshape(TB, 512)
    mine = lax.dynamic_slice(given, (0, core * KH), (TB, KH))
    theirs = partner(lax.dynamic_slice(given, (0, (1 - core) * KH), (TB, KH)))
    left = (jnp.concatenate([mine, theirs], 0).astype(F32) - total).astype(BF16)
    mine, theirs = left[:TB], partner(left[TB:])
    remaining = jnp.where(
        core == 0, jnp.concatenate([mine, theirs], 1), jnp.concatenate([theirs, mine], 1)
    )

    pair1 = lax.dynamic_slice(solved1, (0, jnp.maximum(chip - 8, 0) * 2 * TB), (KH, 2 * TB))
    pair = jnp.where(chip < 8, solved0, pair1)
    mine = lax.dynamic_slice(pair, (0, core * TB), (KH, TB))
    theirs = partner(lax.dynamic_slice(pair, (0, (1 - core) * TB), (KH, TB)))
    solved = jnp.where(
        core == 0, jnp.concatenate([mine, theirs], 0), jnp.concatenate([theirs, mine], 0)
    ).T
    return solved.reshape(1, 1, TB, 512), remaining.reshape(rhs_trail.shape)


def solution(mesh):
    torus = Mesh(mesh.devices.reshape(mesh.shape["row"], 4, 4, 2), ("row", *COL))
    placed = (
        P(None, None, "row", None, None),
        P(None, None, "row", None, None, COL, None),
        P(None, None, "row", None, COL),
        P(None, COL, None, None),
        P(None, "row", None, None, COL, None),
        P(None, "row", None, COL),
        P(COL, None, "row", None, None),
    )
    return jax.shard_map(
        body,
        mesh=torus,
        in_specs=placed,
        out_specs=(P(None, COL, None, None), P(COL, None, "row", None, None)),
        check_vma=False,
    )
```

```python
import jax
import jax.numpy as jnp
from jax import lax
from jax.sharding import Mesh
from jax.sharding import PartitionSpec as P

TB = 128
COL = ("x", "y", "core")
CHIP = ("x", "y")
ROWS = 8
CHIPS = 16
KH = 256
F32 = jnp.float32
BF16 = jnp.bfloat16


def exchange(x, axis):
    return lax.all_to_all(x, axis, split_axis=0, concat_axis=0, tiled=True)


def copies(x, axis, n):
    return exchange(jnp.broadcast_to(x, (n, *x.shape)), axis)


def partner(x):
    return lax.ppermute(x, "core", [(0, 1), (1, 0)])


def shifted(x, axis, step, sources):
    return lax.ppermute(x, axis, [(i, (i + step) % 4) for i in sources])


def dot_nt(a, b):
    return lax.dot_general(a, b, (((1,), (1,)), ((), ())), preferred_element_type=F32)


def natural(x, core):
    return jnp.where(core == 0, x, jnp.roll(x, TB, axis=1))


def placed_at(parts, slots):
    whole = jnp.zeros((len(parts), *parts[0].shape), parts[0].dtype)
    for part, slot in zip(parts, slots):
        whole = lax.dynamic_update_index_in_dim(whole, part, slot, 0)
    return whole


def gathered_in_plane(x, here_x, here_y, first):
    sources = (first, first + 1)
    arrived = [x] + [shifted(x, "x", d, sources) for d in (1, 2, 3)]
    stacked = jnp.stack(arrived)
    pair = jnp.stack(
        [
            lax.dynamic_index_in_dim(stacked, (here_x - s) % 4, 0, keepdims=False)
            for s in sources
        ]
    )
    along = [pair] + [shifted(pair, "y", d, range(4)) for d in (1, 2, 3)]
    return placed_at(along, [(here_y - d) % 4 for d in range(4)])


def tiles_of_rows(tiles, here_x, here_y):
    by_x = tiles.reshape(4, 8, TB, TB)
    sent = [lax.dynamic_index_in_dim(by_x, (here_x + d) % 4, 0, keepdims=False) for d in range(4)]
    came = [sent[0]] + [shifted(sent[d], "x", d, range(4)) for d in (1, 2, 3)]
    by_y = placed_at(came, [(here_x - d) % 4 for d in range(4)]).reshape(4, 4, 2, TB, TB)
    sent = [lax.dynamic_index_in_dim(by_y, (here_y + d) % 4, 1, keepdims=False) for d in range(4)]
    came = [sent[0]] + [shifted(sent[d], "y", d, range(4)) for d in (1, 2, 3)]
    return placed_at(came, [(here_y - d) % 4 for d in range(4)])


def steps(rhs_super, factor_super, mask_super, dinv_rows, factor_trail, mask_trail, rhs_trail):
    core = lax.axis_index("core")
    here_x = lax.axis_index("x")
    here_y = lax.axis_index("y")
    chip = lax.axis_index(CHIP)
    row = lax.axis_index("row")

    rhs0 = rhs_super[0, :, 0].reshape(2 * TB, 512)
    rhs0_t = lax.dynamic_slice(rhs0, (0, core * KH), (2 * TB, KH)).T
    rhs0_t, dinv, factor_trail = lax.optimization_barrier((rhs0_t, dinv_rows[0, 0], factor_trail))
    due0 = exchange(rhs0_t.reshape(ROWS, 32, 2 * TB), "row")
    due0 = due0.reshape(ROWS, 32, 2, TB).transpose(1, 2, 0, 3).reshape(32, 2048)
    dinv_other = partner(dinv)

    keep_trail = mask_trail.astype(BF16).reshape(32, 1, 1)
    tiles = tiles_of_rows(factor_trail.reshape(32, TB, TB) * keep_trail, here_x, here_y)
    d1 = lax.dynamic_index_in_dim(dinv.reshape(TB, 2, ROWS, TB), row, 2, False).reshape(TB, 2 * TB)
    d1_own = gathered_in_plane(d1, here_x, here_y, 2)
    d1_own = d1_own.transpose(1, 0, 2, 3).reshape(8 * TB, 2 * TB)
    d1_other = partner(d1_own)

    solved0 = jnp.concatenate([dot_nt(due0, dinv), dot_nt(due0, dinv_other)], 1).astype(BF16)
    solved0 = copies(solved0, "row", ROWS).reshape(KH, 2 * TB)

    keep = mask_super[1].astype(BF16).reshape(2, 1, 1)
    tiles10 = (factor_super[1].reshape(2, TB, TB) * keep).reshape(2 * TB, TB)
    tiles10 = jnp.concatenate([tiles10, partner(tiles10)], 1)
    reached = dot_nt(solved0, tiles10)
    reached = exchange(reached.reshape(CHIPS, 16, 2 * TB), CHIP)[:8].sum(0)
    rhs1 = rhs_super[1, :, 0].reshape(2 * TB, 512)
    rhs1_t = lax.dynamic_slice(rhs1, (0, core * KH + chip * 16), (2 * TB, 16)).T
    due1 = (rhs1_t.astype(F32) - reached).astype(BF16)

    part = jnp.concatenate(
        [dot_nt(due1, d1_own).reshape(16, 8, TB), dot_nt(due1, d1_other).reshape(16, 8, TB)], 2
    ).transpose(1, 0, 2)
    solved1 = exchange(part, "row").sum(0).astype(BF16)
    solved1 = copies(natural(solved1, core), "row", ROWS)
    solved1 = solved1.transpose(1, 0, 2).reshape(16, 2048)
    solved1 = copies(solved1, CHIP, CHIPS).reshape(KH, 2048)

    both = jnp.where(
        core == 0, jnp.stack([tiles, partner(tiles)]), jnp.stack([partner(tiles), tiles])
    )
    both = both.transpose(3, 4, 2, 1, 0, 5).reshape(2 * TB, 4096)
    solved0 = lax.optimization_barrier(natural(solved0, core))
    all0 = gathered_in_plane(solved0, here_x, here_y, 0)
    all0 = all0.transpose(2, 1, 0, 3).reshape(KH, 2048)
    early = lax.optimization_barrier(dot_nt(both[:, :2048], all0))
    total = early + dot_nt(both[:, 2048:], solved1)
    given = rhs_trail.reshape(TB, 512)
    mine = lax.dynamic_slice(given, (0, core * KH), (TB, KH))
    theirs = partner(lax.dynamic_slice(given, (0, (1 - core) * KH), (TB, KH)))
    mine = mine.astype(F32) - total_rows(total, core)
    theirs = theirs.astype(F32) - total_rows(total, 1 - core)
    mine, theirs = mine.astype(BF16), partner(theirs.astype(BF16))
    remaining = jnp.where(
        core == 0, jnp.concatenate([mine, theirs], 1), jnp.concatenate([theirs, mine], 1)
    )

    pair1 = lax.dynamic_slice(solved1, (0, jnp.maximum(chip - 8, 0) * 2 * TB), (KH, 2 * TB))
    pair = jnp.where(chip < 8, solved0, pair1)
    mine = lax.dynamic_slice(pair, (0, core * TB), (KH, TB))
    theirs = partner(lax.dynamic_slice(pair, (0, (1 - core) * TB), (KH, TB)))
    solved = jnp.where(
        core == 0, jnp.concatenate([mine, theirs], 0), jnp.concatenate([theirs, mine], 0)
    ).T
    return solved.reshape(1, 1, TB, 512), remaining.reshape(rhs_trail.shape)


def total_rows(total, which):
    return lax.dynamic_slice(total, (which * TB, 0), (TB, KH))


def solution(mesh):
    torus = Mesh(mesh.devices.reshape(mesh.shape["row"], 4, 4, 2), ("row", *COL))
    placed = (
        P(None, None, "row", None, None),
        P(None, None, "row", None, None, COL, None),
        P(None, None, "row", None, COL),
        P(None, COL, None, None),
        P(None, "row", None, None, COL, None),
        P(None, "row", None, COL),
        P(COL, None, "row", None, None),
    )
    return jax.shard_map(
        steps,
        mesh=torus,
        in_specs=placed,
        out_specs=(P(None, COL, None, None), P(COL, None, "row", None, None)),
        check_vma=False,
    )
```

```python
import functools
import math

import jax
import jax.numpy as jnp
from jax import lax
from jax.experimental import pallas as pl
from jax.experimental.pallas import tpu as pltpu
from jax.sharding import Mesh
from jax.sharding import PartitionSpec as P


TB = 128
COL = ("x", "y", "core")
CHIP = ("x", "y")
ROWS = 8
CHIPS = 16
K = 512
F32 = jnp.float32
BF16 = jnp.bfloat16
SHIFTS = (0, 1, 2, 3)


def exchange(x, axis):
    return lax.all_to_all(x, axis, split_axis=0, concat_axis=0, tiled=True)


def partner(x):
    return lax.ppermute(x, "core", [(0, 1), (1, 0)])


def shifted(x, axis, step, sources):
    return lax.ppermute(x, axis, [(i, (i + step) % 4) for i in sources])


def dot_nt(a, b):
    return lax.dot_general(a, b, (((1,), (1,)), ((), ())), preferred_element_type=F32)


def here():
    return lax.axis_index("x"), lax.axis_index("y")


def back(index, step):
    return lax.rem(index - step + 4, 4)


def local(kernel, outs, *args, smem=(), flops=1_000_000):
    size = sum(a.size * a.dtype.itemsize for a in args)
    kept = size + sum(math.prod(shape) * jnp.dtype(dtype).itemsize for shape, dtype in outs)
    specs = [
        pl.BlockSpec(memory_space=pltpu.SMEM if i in smem else pltpu.VMEM)
        for i in range(len(args))
    ]
    return pl.pallas_call(
        kernel,
        out_shape=[jax.ShapeDtypeStruct(shape, dtype) for shape, dtype in outs],
        in_specs=specs,
        out_specs=[pl.BlockSpec(memory_space=pltpu.VMEM) for _ in outs],
        cost_estimate=pl.CostEstimate(flops=flops, bytes_accessed=2 * size, transcendentals=0),
        compiler_params=pltpu.CompilerParams(vmem_limit_bytes=kept + 2**21),
    )(*args)


def turned(given, out):
    lines = jnp.concatenate([given[0, 0, 0].T, given[0, 1, 0].T], axis=1)
    lines = lines.reshape(16, 2, 16, 2 * TB)
    lines = jnp.where(lax.axis_index("core") == 0, lines[:, 0], lines[:, 1])
    out[...] = lines.reshape(ROWS, 32, 2 * TB)


def send_x(factor, mask, *outs):
    x, _ = here()
    for d, out in enumerate(outs):
        base = lax.rem(x + d, 4) * 8
        for i in range(8):
            out[i] = jnp.where(mask[base + i] == 1, factor[base + i], jnp.zeros((TB, TB), BF16))


def pack_y(*refs):
    came, outs = refs[:4], refs[4:]
    _, y = here()
    for e, out in enumerate(outs):
        base = lax.rem(y + e, 4) * 2
        for d in SHIFTS:
            out[2 * d] = came[d][base]
            out[2 * d + 1] = came[d][base + 1]


def pick(first, *refs):
    came, out = refs[:4], refs[4]
    x, _ = here()
    for d in SHIFTS:
        side = back(x, d) - first

        @pl.when(jnp.logical_and(side >= 0, side < 2))
        def _(d=d, side=side):
            out[side] = came[d][...]


def first_rows(due, own, other, out):
    lines = jnp.concatenate(
        [due[r][:, a * TB : (a + 1) * TB] for a in range(2) for r in range(ROWS)], axis=1
    )
    both = jnp.concatenate([dot_nt(lines, own[...]), dot_nt(lines, other[...])], axis=1)
    both = both.astype(BF16)
    for r in range(ROWS):
        out[r] = both


def update(solved, own, other, out):
    tiles = jnp.concatenate([own[...], other[...]], axis=1)
    reached = dot_nt(solved[...].reshape(256, 256), tiles)
    out[...] = reached.reshape(CHIPS, 16, 2 * TB)


def due_rows(came, given, out):
    reached = came[0]
    for chip in range(1, 8):
        reached = reached + came[chip]
    out[...] = (given[...].astype(F32) - reached).astype(BF16)


def second_rows(mine, theirs, *refs):
    pieces, out = refs[:4], refs[4]
    _, y = here()
    first = lax.axis_index("core") == 0
    a, b = mine[...], theirs[...]
    due = jnp.concatenate([jnp.where(first, a, b), jnp.where(first, b, a)], axis=0)
    for e in SHIFTS:
        for side in range(2):
            out[side * 4 + back(y, e)] = dot_nt(due, pieces[e][side])


def spread(given, out):
    for chip in range(CHIPS):
        out[chip] = given[...]


def second_sum(came, out):
    total = came[0]
    for r in range(1, ROWS):
        total = total + came[r]
    total = total.astype(BF16)
    for r in range(ROWS):
        out[r] = total


def early_part(*refs):
    tiles, solved, out = refs[:4], refs[4:8], refs[8]
    x, _ = here()
    total = jnp.zeros((2 * TB, K), F32)
    for e in SHIFTS:
        for side in range(2):
            block = tiles[e][pl.ds(back(x, side) * 2, 2)].reshape(2 * TB, TB)
            total = total + dot_nt(block, solved[e][side])
    out[...] = total.reshape(2, TB, K)


def late_part(tiles, solved, which):
    x, y = here()
    total = jnp.zeros((TB, K), F32)
    for e in SHIFTS:
        for side in range(2):
            block = tiles[e][back(x, 2 + side) * 2 + which]
            lines = solved[:, side * 4 + back(y, e)].reshape(K, TB)
            total = total + dot_nt(block, lines)
    return total


def part_of_partner(*refs):
    tiles, solved, early, out = refs[:4], *refs[4:]
    which = 1 - lax.axis_index("core")
    out[...] = early[which] + late_part(tiles, solved, which)


def own_part(*refs):
    tiles, solved, early, solved0, given, left, result = refs[:4], *refs[4:]
    which = lax.axis_index("core")
    left[...] = given[...].astype(F32) - (early[which] + late_part(tiles, solved, which))
    chip = lax.axis_index("x") * 4 + lax.axis_index("y")

    @pl.when(chip < 8)
    def _():
        result[...] = solved0[...].T

    @pl.when(chip >= 8)
    def _():
        result[...] = solved[:, chip - 8].reshape(K, TB).T


def steps(rhs_super, factor_super, mask_super, dinv_rows, factor_trail, mask_trail, rhs_trail):
    core = lax.axis_index("core")
    chip = lax.axis_index(CHIP)

    rhs0 = pl.pallas_call(
        turned,
        grid=(1,),
        out_shape=jax.ShapeDtypeStruct((ROWS, 32, 2 * TB), BF16),
        in_specs=[pl.BlockSpec((1, 2, 1, TB, K), lambda i: (0, 0, 0, 0, 0))],
        out_specs=pl.BlockSpec((ROWS, 32, 2 * TB), lambda i: (0, 0, 0)),
        compiler_params=pltpu.CompilerParams(vmem_limit_bytes=2**22),
        name="turn",
    )(rhs_super)
    rhs0, dinv, factor_trail, rhs_super = lax.optimization_barrier(
        (rhs0, dinv_rows[0, 0], factor_trail, rhs_super)
    )
    due0 = exchange(rhs0, "row")
    dinv_other = partner(dinv)
    row = lax.axis_index("row")
    d1 = jnp.concatenate(
        [lax.dynamic_slice(dinv, (0, (a * ROWS + row) * TB), (TB, TB)) for a in range(2)], 1
    )
    came = [d1] + [shifted(d1, "x", d, (2, 3)) for d in (1, 2, 3)]
    [d1] = local(functools.partial(pick, 2), [((2, TB, 2 * TB), BF16)], *came)
    d1 = [d1] + [shifted(d1, "y", e, SHIFTS) for e in (1, 2, 3)]

    mask = mask_trail.reshape(32)
    sent = local(
        send_x, [((8, TB, TB), BF16)] * 4, factor_trail.reshape(32, TB, TB), mask,
        smem=(1,),
    )
    came = [sent[0]] + [shifted(sent[d], "x", d, SHIFTS) for d in (1, 2, 3)]
    sent = local(pack_y, [((8, TB, TB), BF16)] * 4, *came)
    tiles = [sent[0]] + [shifted(sent[e], "y", e, SHIFTS) for e in (1, 2, 3)]

    [solved0] = local(
        first_rows, [((ROWS, 32, 2 * TB), BF16)], due0, dinv, dinv_other,
        flops=2**26,
    )
    solved0 = exchange(solved0, "row")

    keep = mask_super[1].astype(BF16).reshape(2, 1, 1)
    tiles10 = (factor_super[1].reshape(2, TB, TB) * keep).reshape(2 * TB, TB)
    [reached] = local(
        update, [((CHIPS, 16, 2 * TB), F32)], solved0, tiles10, partner(tiles10),
        flops=2**25,
    )
    reached = exchange(reached, CHIP)
    rhs1 = rhs_super[1, :, 0].reshape(2 * TB, K)
    rhs1 = lax.dynamic_slice(rhs1, (0, chip * 32 + core * 16), (2 * TB, 16)).T
    [due1] = local(due_rows, [((16, 2 * TB), BF16)], reached, rhs1)
    [part] = local(
        second_rows, [((ROWS, 32, TB), F32)], due1, partner(due1), *d1,
        flops=2**25,
    )
    part = exchange(part, "row")
    [solved1] = local(second_sum, [((ROWS, 32, TB), BF16)], part)
    solved1 = exchange(solved1, "row")
    [solved1] = local(spread, [((CHIPS, ROWS, 32, TB), BF16)], solved1)
    solved1 = exchange(solved1, CHIP)

    pairs = solved0.reshape(2 * K // 4, 2 * TB)
    mine, theirs = pairs[:, :TB], partner(pairs[:, TB:])
    mine, theirs = mine.reshape(16, 16, TB), theirs.reshape(16, 16, TB)
    own0 = jnp.where(
        core == 0, jnp.stack([mine, theirs], 1), jnp.stack([theirs, mine], 1)
    ).reshape(K, TB)
    came = [own0] + [shifted(own0, "x", d, (0, 1)) for d in (1, 2, 3)]
    [pair] = local(functools.partial(pick, 0), [((2, K, TB), BF16)], *came)
    all0 = [pair] + [shifted(pair, "y", e, SHIFTS) for e in (1, 2, 3)]

    [early] = local(early_part, [((2, TB, K), F32)], *tiles, *all0, flops=2**28)
    [theirs] = local(part_of_partner, [((TB, K), F32)], *tiles, solved1, early, flops=2**27)
    theirs = partner(theirs)
    left, solved = local(
        own_part, [((TB, K), F32), ((TB, K), BF16)], *tiles, solved1, early, own0,
        rhs_trail.reshape(TB, K), flops=2**27,
    )
    remaining = (left - theirs).astype(BF16)
    return solved.reshape(1, 1, TB, K), remaining.reshape(rhs_trail.shape)


def solution(mesh):
    torus = Mesh(mesh.devices.reshape(mesh.shape["row"], 4, 4, 2), ("row", *COL))
    placed = (
        P(None, None, "row", None, None),
        P(None, None, "row", None, None, COL, None),
        P(None, None, "row", None, COL),
        P(None, COL, None, None),
        P(None, "row", None, None, COL, None),
        P(None, "row", None, COL),
        P(COL, None, "row", None, None),
    )
    return jax.shard_map(
        steps,
        mesh=torus,
        in_specs=placed,
        out_specs=(P(None, COL, None, None), P(COL, None, "row", None, None)),
        check_vma=False,
    )
```

```python
import functools
import math

import jax
import jax.numpy as jnp
from jax import lax
from jax.experimental import pallas as pl
from jax.experimental.pallas import tpu as pltpu
from jax.sharding import Mesh
from jax.sharding import PartitionSpec as P


TB = 128
COL = ("x", "y", "core")
CHIP = ("x", "y")
ROWS = 8
CHIPS = 16
K = 512
F32 = jnp.float32
BF16 = jnp.bfloat16
SHIFTS = (0, 1, 2, 3)


def exchange(x, axis):
    return lax.all_to_all(x, axis, split_axis=0, concat_axis=0, tiled=True)


def partner(x):
    return lax.ppermute(x, "core", [(0, 1), (1, 0)])


def shifted(x, axis, step, sources):
    return lax.ppermute(x, axis, [(i, (i + step) % 4) for i in sources])


def crossed(x, step, phase):
    pairs = []
    for i in range(32):
        at = [i // 8, i // 2 % 4, i % 2]
        at[(i + phase) % 2] = (at[(i + phase) % 2] + step) % 4
        pairs.append((i, at[0] * 8 + at[1] * 2 + at[2]))
    return lax.ppermute(x, COL, pairs)


def crossed_here():
    first = lax.axis_index("core") == 0
    x, y = here()
    return jnp.where(first, x, y), jnp.where(first, y, x), first


def dot_nt(a, b):
    return lax.dot_general(a, b, (((1,), (1,)), ((), ())), preferred_element_type=F32)


def here():
    return lax.axis_index("x"), lax.axis_index("y")


def back(index, step):
    return lax.rem(index - step + 4, 4)


def local(kernel, outs, *args, smem=(), flops=1_000_000):
    size = sum(a.size * a.dtype.itemsize for a in args)
    kept = size + sum(math.prod(shape) * jnp.dtype(dtype).itemsize for shape, dtype in outs)
    specs = [
        pl.BlockSpec(memory_space=pltpu.SMEM if i in smem else pltpu.VMEM)
        for i in range(len(args))
    ]
    return pl.pallas_call(
        kernel,
        out_shape=[jax.ShapeDtypeStruct(shape, dtype) for shape, dtype in outs],
        in_specs=specs,
        out_specs=[pl.BlockSpec(memory_space=pltpu.VMEM) for _ in outs],
        cost_estimate=pl.CostEstimate(flops=flops, bytes_accessed=2 * size, transcendentals=0),
        compiler_params=pltpu.CompilerParams(vmem_limit_bytes=kept + 2**21),
    )(*args)


def turned(given, out):
    lines = jnp.concatenate([given[0, 0, 0].T, given[0, 1, 0].T], axis=1)
    lines = lines.reshape(16, 2, 16, 2 * TB)
    lines = jnp.where(lax.axis_index("core") == 0, lines[:, 0], lines[:, 1])
    out[...] = lines.reshape(ROWS, 32, 2 * TB)


def send_first(factor, mask, *outs):
    u, _, first = crossed_here()
    far, near = jnp.where(first, 8, 2), jnp.where(first, 2, 8)
    for d, out in enumerate(outs):
        base = lax.rem(u + d, 4) * far
        for v in range(4):
            for kk in range(2):
                t = base + v * near + kk
                out[2 * v + kk] = jnp.where(mask[t] == 1, factor[t], jnp.zeros((TB, TB), BF16))


def send_second(*refs):
    came, outs = refs[:4], refs[4:]
    _, v, _ = crossed_here()
    for e, out in enumerate(outs):
        base = lax.rem(v + e, 4) * 2
        for d in SHIFTS:
            out[2 * d] = came[d][base]
            out[2 * d + 1] = came[d][base + 1]


def pick(first, *refs):
    came, out = refs[:4], refs[4]
    x, _ = here()
    for d in SHIFTS:
        side = back(x, d) - first

        @pl.when(jnp.logical_and(side >= 0, side < 2))
        def _(d=d, side=side):
            out[side] = came[d][...]


def first_rows(due, own, other, out):
    lines = jnp.concatenate(
        [due[r][:, a * TB : (a + 1) * TB] for a in range(2) for r in range(ROWS)], axis=1
    )
    both = jnp.concatenate([dot_nt(lines, own[...]), dot_nt(lines, other[...])], axis=1)
    both = both.astype(BF16)
    for r in range(ROWS):
        out[r] = both


def update(solved, own, other, out):
    tiles = jnp.concatenate([own[...], other[...]], axis=1)
    reached = dot_nt(solved[...].reshape(256, 256), tiles)
    out[...] = reached.reshape(CHIPS, 16, 2 * TB)


def due_rows(came, given, out):
    reached = came[0]
    for chip in range(1, 8):
        reached = reached + came[chip]
    out[...] = (given[...].astype(F32) - reached).astype(BF16)


def second_rows(mine, theirs, *refs):
    pieces, out = refs[:4], refs[4]
    _, y = here()
    first = lax.axis_index("core") == 0
    a, b = mine[...], theirs[...]
    due = jnp.concatenate([jnp.where(first, a, b), jnp.where(first, b, a)], axis=0)
    for e in SHIFTS:
        for side in range(2):
            out[side * 4 + back(y, e)] = dot_nt(due, pieces[e][side])


def pack_lines(*refs):
    came, out = refs[:4], refs[4]
    u, _, _ = crossed_here()
    for d in SHIFTS:
        out[back(u, d)] = came[d][...]


def second_sum(came, out):
    total = came[0]
    for r in range(1, ROWS):
        total = total + came[r]
    total = total.astype(BF16)
    for r in range(ROWS):
        out[r] = total


def early_part(*refs):
    came, solved, out, tiles = refs[:4], refs[4:8], *refs[8:]
    _, y = here()
    u, v, first = crossed_here()
    for e in SHIFTS:
        for d in SHIFTS:
            at_u, at_v = back(u, d), back(v, e)
            tiles[jnp.where(first, at_u * 4 + at_v, at_v * 4 + at_u)] = came[e][2 * d : 2 * d + 2]
    total = jnp.zeros((2 * TB, K), F32)
    for e in SHIFTS:
        for side in range(2):
            block = tiles[side * 4 + back(y, e)].reshape(2 * TB, TB)
            total = total + dot_nt(block, solved[e][side])
    out[...] = total.reshape(2, TB, K)


def late_part(tiles, solved, which):
    total = jnp.zeros((TB, K), F32)
    for tile in range(8):
        total = total + dot_nt(tiles[8 + tile, which], solved[:, tile].reshape(K, TB))
    return total


def part_of_partner(*refs):
    tiles, pieces, early, out, solved = refs[0], refs[1:5], *refs[5:]
    _, v, first = crossed_here()
    for e in SHIFTS:
        source = back(v, e)
        for u in range(4):
            solved[jnp.where(first, u * 4 + source, source * 4 + u)] = pieces[e][u]
    which = 1 - lax.axis_index("core")
    out[...] = early[which] + late_part(tiles, solved, which)


def own_part(tiles, solved, early, solved0, given, left, result):
    which = lax.axis_index("core")
    left[...] = given[...].astype(F32) - (early[which] + late_part(tiles, solved, which))
    chip = lax.axis_index("x") * 4 + lax.axis_index("y")

    @pl.when(chip < 8)
    def _():
        result[...] = solved0[...].T

    @pl.when(chip >= 8)
    def _():
        result[...] = solved[:, chip - 8].reshape(K, TB).T


def steps(rhs_super, factor_super, mask_super, dinv_rows, factor_trail, mask_trail, rhs_trail):
    core = lax.axis_index("core")
    chip = lax.axis_index(CHIP)

    rhs0 = pl.pallas_call(
        turned,
        grid=(1,),
        out_shape=jax.ShapeDtypeStruct((ROWS, 32, 2 * TB), BF16),
        in_specs=[pl.BlockSpec((1, 2, 1, TB, K), lambda i: (0, 0, 0, 0, 0))],
        out_specs=pl.BlockSpec((ROWS, 32, 2 * TB), lambda i: (0, 0, 0)),
        compiler_params=pltpu.CompilerParams(vmem_limit_bytes=62 * 2**20),
        name="turn",
    )(rhs_super)
    rhs0, dinv, factor_trail, rhs_super = lax.optimization_barrier(
        (rhs0, dinv_rows[0, 0], factor_trail, rhs_super)
    )
    due0 = exchange(rhs0, "row")
    dinv_other = partner(dinv)
    row = lax.axis_index("row")
    d1 = jnp.concatenate(
        [lax.dynamic_slice(dinv, (0, (a * ROWS + row) * TB), (TB, TB)) for a in range(2)], 1
    )
    came = [d1] + [shifted(d1, "x", d, SHIFTS) for d in (1, 2, 3)]
    [d1] = local(functools.partial(pick, 2), [((2, TB, 2 * TB), BF16)], *came)
    d1 = [d1] + [shifted(d1, "y", e, SHIFTS) for e in (1, 2, 3)]

    mask = mask_trail.reshape(32)
    sent = local(
        send_first, [((8, TB, TB), BF16)] * 4, factor_trail.reshape(32, TB, TB), mask,
        smem=(1,),
    )
    came = [sent[0]] + [crossed(sent[d], d, 0) for d in (1, 2, 3)]
    sent = local(send_second, [((8, TB, TB), BF16)] * 4, *came)
    tiles = [sent[0]] + [crossed(sent[e], e, 1) for e in (1, 2, 3)]

    [solved0] = local(
        first_rows, [((ROWS, 32, 2 * TB), BF16)], due0, dinv, dinv_other,
        flops=2**26,
    )
    solved0 = exchange(solved0, "row")

    keep = mask_super[1].astype(BF16).reshape(2, 1, 1)
    tiles10 = (factor_super[1].reshape(2, TB, TB) * keep).reshape(2 * TB, TB)
    [reached] = local(
        update, [((CHIPS, 16, 2 * TB), F32)], solved0, tiles10, partner(tiles10),
        flops=2**25,
    )
    reached = exchange(reached, CHIP)
    rhs1 = rhs_super[1, :, 0].reshape(2 * TB, K)
    rhs1 = lax.dynamic_slice(rhs1, (0, chip * 32 + core * 16), (2 * TB, 16)).T
    [due1] = local(due_rows, [((16, 2 * TB), BF16)], reached, rhs1)
    [part] = local(
        second_rows, [((ROWS, 32, TB), F32)], due1, partner(due1), *d1,
        flops=2**25,
    )
    part = exchange(part, "row")
    [solved1] = local(second_sum, [((ROWS, 32, TB), BF16)], part)
    solved1 = exchange(solved1, "row")
    came = {d: crossed(solved1, d, 0) for d in (2, 1, 3)}
    [lines] = local(pack_lines, [((4, ROWS, 32, TB), BF16)], solved1, came[1], came[2], came[3])
    came = {e: crossed(lines, e, 1) for e in (2, 1, 3)}
    pieces = [lines, came[1], came[2], came[3]]

    pairs = solved0.reshape(2 * K // 4, 2 * TB)
    mine, theirs = pairs[:, :TB], partner(pairs[:, TB:])
    mine, theirs = mine.reshape(16, 16, TB), theirs.reshape(16, 16, TB)
    own0 = jnp.where(
        core == 0, jnp.stack([mine, theirs], 1), jnp.stack([theirs, mine], 1)
    ).reshape(K, TB)
    came = [own0] + [shifted(own0, "x", d, SHIFTS) for d in (1, 2, 3)]
    [pair] = local(functools.partial(pick, 0), [((2, K, TB), BF16)], *came)
    all0 = [pair] + [shifted(pair, "y", e, SHIFTS) for e in (1, 2, 3)]

    early, tiles = local(
        early_part, [((2, TB, K), F32), ((CHIPS, 2, TB, TB), BF16)], *tiles, *all0,
        flops=2**28,
    )
    theirs, solved1 = local(
        part_of_partner, [((TB, K), F32), ((CHIPS, ROWS, 32, TB), BF16)], tiles, *pieces, early,
        flops=2**27,
    )
    theirs = partner(theirs)
    left, solved = local(
        own_part, [((TB, K), F32), ((TB, K), BF16)], tiles, solved1, early, own0,
        rhs_trail.reshape(TB, K), flops=2**27,
    )
    remaining = (left - theirs).astype(BF16)
    return solved.reshape(1, 1, TB, K), remaining.reshape(rhs_trail.shape)


def solution(mesh):
    torus = Mesh(mesh.devices.reshape(mesh.shape["row"], 4, 4, 2), ("row", *COL))
    placed = (
        P(None, None, "row", None, None),
        P(None, None, "row", None, None, COL, None),
        P(None, None, "row", None, COL),
        P(None, COL, None, None),
        P(None, "row", None, None, COL, None),
        P(None, "row", None, COL),
        P(COL, None, "row", None, None),
    )
    return jax.shard_map(
        steps,
        mesh=torus,
        in_specs=placed,
        out_specs=(P(None, COL, None, None), P(COL, None, "row", None, None)),
        check_vma=False,
    )
```

```python
import functools
import math

import jax
import jax.numpy as jnp
from jax import lax
from jax.experimental import pallas as pl
from jax.experimental.pallas import tpu as pltpu
from jax.sharding import Mesh
from jax.sharding import PartitionSpec as P


TB = 128
COL = ("x", "y", "core")
CHIP = ("x", "y")
ROWS = 8
CHIPS = 16
K = 512
F32 = jnp.float32
BF16 = jnp.bfloat16
SHIFTS = (0, 1, 2, 3)


def exchange(x, axis):
    return lax.all_to_all(x, axis, split_axis=0, concat_axis=0, tiled=True)


def partner(x):
    return lax.ppermute(x, "core", [(0, 1), (1, 0)])


def shifted(x, axis, step, sources):
    return lax.ppermute(x, axis, [(i, (i + step) % 4) for i in sources])


def crossed_groups():
    groups = []
    for core in range(2):
        for other in range(4):
            group = []
            for along in range(4):
                x, y = (along, other) if core == 0 else (other, along)
                group += [r * 32 + x * 8 + y * 2 + core for r in range(ROWS)]
            groups.append(group)
    return groups


def crossed(x, step, phase):
    pairs = []
    for i in range(32):
        at = [i // 8, i // 2 % 4, i % 2]
        at[(i + phase) % 2] = (at[(i + phase) % 2] + step) % 4
        pairs.append((i, at[0] * 8 + at[1] * 2 + at[2]))
    return lax.ppermute(x, COL, pairs)


def crossed_here():
    first = lax.axis_index("core") == 0
    x, y = here()
    return jnp.where(first, x, y), jnp.where(first, y, x), first


def dot_nt(a, b):
    return lax.dot_general(a, b, (((1,), (1,)), ((), ())), preferred_element_type=F32)


def here():
    return lax.axis_index("x"), lax.axis_index("y")


def back(index, step):
    return lax.rem(index - step + 4, 4)


def local(kernel, outs, *args, smem=(), flops=1_000_000):
    size = sum(a.size * a.dtype.itemsize for a in args)
    kept = size + sum(math.prod(shape) * jnp.dtype(dtype).itemsize for shape, dtype in outs)
    specs = [
        pl.BlockSpec(memory_space=pltpu.SMEM if i in smem else pltpu.VMEM)
        for i in range(len(args))
    ]
    return pl.pallas_call(
        kernel,
        out_shape=[jax.ShapeDtypeStruct(shape, dtype) for shape, dtype in outs],
        in_specs=specs,
        out_specs=[pl.BlockSpec(memory_space=pltpu.VMEM) for _ in outs],
        cost_estimate=pl.CostEstimate(flops=flops, bytes_accessed=2 * size, transcendentals=0),
        compiler_params=pltpu.CompilerParams(vmem_limit_bytes=kept + 2**21),
    )(*args)


def turned(given, out):
    lines = jnp.concatenate([given[0, 0, 0].T, given[0, 1, 0].T], axis=1)
    lines = lines.reshape(16, 2, 16, 2 * TB)
    lines = jnp.where(lax.axis_index("core") == 0, lines[:, 0], lines[:, 1])
    out[...] = lines.reshape(ROWS, 32, 2 * TB)


def send_first(factor, mask, *outs):
    u, _, first = crossed_here()
    far, near = jnp.where(first, 8, 2), jnp.where(first, 2, 8)
    for d, out in enumerate(outs):
        base = lax.rem(u + d, 4) * far
        for v in range(4):
            for kk in range(2):
                t = base + v * near + kk
                out[2 * v + kk] = jnp.where(mask[t] == 1, factor[t], jnp.zeros((TB, TB), BF16))


def send_second(*refs):
    came, outs = refs[:4], refs[4:]
    _, v, _ = crossed_here()
    for e, out in enumerate(outs):
        base = lax.rem(v + e, 4) * 2
        for d in SHIFTS:
            out[2 * d] = came[d][base]
            out[2 * d + 1] = came[d][base + 1]


def pick(first, *refs):
    came, out = refs[:4], refs[4]
    x, _ = here()
    for d in SHIFTS:
        side = back(x, d) - first

        @pl.when(jnp.logical_and(side >= 0, side < 2))
        def _(d=d, side=side):
            out[side] = came[d][...]


def first_rows(due, own, other, out):
    lines = jnp.concatenate(
        [due[r][:, a * TB : (a + 1) * TB] for a in range(2) for r in range(ROWS)], axis=1
    )
    both = jnp.concatenate([dot_nt(lines, own[...]), dot_nt(lines, other[...])], axis=1)
    both = both.astype(BF16)
    for r in range(ROWS):
        out[r] = both


def update(solved, own, other, out):
    tiles = jnp.concatenate([own[...], other[...]], axis=1)
    reached = dot_nt(solved[...].reshape(256, 256), tiles)
    out[...] = reached.reshape(CHIPS, 16, 2 * TB)


def due_rows(came, given, out):
    reached = came[0]
    for chip in range(1, 8):
        reached = reached + came[chip]
    out[...] = (given[...].astype(F32) - reached).astype(BF16)


def second_rows(mine, theirs, *refs):
    pieces, out = refs[:4], refs[4]
    _, y = here()
    first = lax.axis_index("core") == 0
    a, b = mine[...], theirs[...]
    due = jnp.concatenate([jnp.where(first, a, b), jnp.where(first, b, a)], axis=0)
    for e in SHIFTS:
        for side in range(2):
            out[side * 4 + back(y, e)] = dot_nt(due, pieces[e][side])


def second_sum(came, out):
    total = came[0]
    for r in range(1, ROWS):
        total = total + came[r]
    total = total.astype(BF16)
    for place in range(4 * ROWS):
        out[place] = total


def early_part(*refs):
    came, solved, out, tiles = refs[:4], refs[4:8], *refs[8:]
    _, y = here()
    u, v, first = crossed_here()
    for e in SHIFTS:
        for d in SHIFTS:
            at_u, at_v = back(u, d), back(v, e)
            tiles[jnp.where(first, at_u * 4 + at_v, at_v * 4 + at_u)] = came[e][2 * d : 2 * d + 2]
    total = jnp.zeros((2 * TB, K), F32)
    for e in SHIFTS:
        for side in range(2):
            block = tiles[side * 4 + back(y, e)].reshape(2 * TB, TB)
            total = total + dot_nt(block, solved[e][side])
    out[...] = total.reshape(2, TB, K)


def late_part(tiles, solved, which):
    total = jnp.zeros((TB, K), F32)
    for tile in range(8):
        total = total + dot_nt(tiles[8 + tile, which], solved[:, tile].reshape(K, TB))
    return total


def part_of_partner(*refs):
    tiles, pieces, early, out, solved = refs[0], refs[1:5], *refs[5:]
    _, v, first = crossed_here()
    for e in SHIFTS:
        source = back(v, e)
        for u in range(4):
            solved[jnp.where(first, u * 4 + source, source * 4 + u)] = pieces[e][u]
    which = 1 - lax.axis_index("core")
    out[...] = early[which] + late_part(tiles, solved, which)


def own_part(tiles, solved, early, solved0, given, left, result):
    which = lax.axis_index("core")
    left[...] = given[...].astype(F32) - (early[which] + late_part(tiles, solved, which))
    chip = lax.axis_index("x") * 4 + lax.axis_index("y")

    @pl.when(chip < 8)
    def _():
        result[...] = solved0[...].T

    @pl.when(chip >= 8)
    def _():
        result[...] = solved[:, chip - 8].reshape(K, TB).T


def steps(rhs_super, factor_super, mask_super, dinv_rows, factor_trail, mask_trail, rhs_trail):
    core = lax.axis_index("core")
    chip = lax.axis_index(CHIP)

    rhs0 = pl.pallas_call(
        turned,
        grid=(1,),
        out_shape=jax.ShapeDtypeStruct((ROWS, 32, 2 * TB), BF16),
        in_specs=[pl.BlockSpec((1, 2, 1, TB, K), lambda i: (0, 0, 0, 0, 0))],
        out_specs=pl.BlockSpec((ROWS, 32, 2 * TB), lambda i: (0, 0, 0)),
        compiler_params=pltpu.CompilerParams(vmem_limit_bytes=62 * 2**20),
        name="turn",
    )(rhs_super)
    rhs0, dinv, factor_trail, rhs_super = lax.optimization_barrier(
        (rhs0, dinv_rows[0, 0], factor_trail, rhs_super)
    )
    due0 = exchange(rhs0, "row")
    dinv_other = partner(dinv)
    row = lax.axis_index("row")
    d1 = jnp.concatenate(
        [lax.dynamic_slice(dinv, (0, (a * ROWS + row) * TB), (TB, TB)) for a in range(2)], 1
    )
    came = [d1] + [shifted(d1, "x", d, SHIFTS) for d in (1, 2, 3)]
    [d1] = local(functools.partial(pick, 2), [((2, TB, 2 * TB), BF16)], *came)
    d1 = [d1] + [shifted(d1, "y", e, SHIFTS) for e in (1, 2, 3)]

    mask = mask_trail.reshape(32)
    sent = local(
        send_first, [((8, TB, TB), BF16)] * 4, factor_trail.reshape(32, TB, TB), mask,
        smem=(1,),
    )
    came = [sent[0]] + [crossed(sent[d], d, 0) for d in (1, 2, 3)]
    sent = local(send_second, [((8, TB, TB), BF16)] * 4, *came)
    tiles = [sent[0]] + [crossed(sent[e], e, 1) for e in (1, 2, 3)]

    [solved0] = local(
        first_rows, [((ROWS, 32, 2 * TB), BF16)], due0, dinv, dinv_other,
        flops=2**26,
    )
    solved0 = exchange(solved0, "row")

    keep = mask_super[1].astype(BF16).reshape(2, 1, 1)
    tiles10 = (factor_super[1].reshape(2, TB, TB) * keep).reshape(2 * TB, TB)
    [reached] = local(
        update, [((CHIPS, 16, 2 * TB), F32)], solved0, tiles10, partner(tiles10),
        flops=2**25,
    )
    reached = exchange(reached, CHIP)
    rhs1 = rhs_super[1, :, 0].reshape(2 * TB, K)
    rhs1 = lax.dynamic_slice(rhs1, (0, chip * 32 + core * 16), (2 * TB, 16)).T
    [due1] = local(due_rows, [((16, 2 * TB), BF16)], reached, rhs1)
    [part] = local(
        second_rows, [((ROWS, 32, TB), F32)], due1, partner(due1), *d1,
        flops=2**25,
    )
    part = exchange(part, "row")
    [solved1] = local(second_sum, [((4 * ROWS, 32, TB), BF16)], part)
    lines = lax.all_to_all(
        solved1, ("row", *COL), 0, 0, axis_index_groups=crossed_groups(), tiled=True
    ).reshape(4, ROWS, 32, TB)
    came = {e: crossed(lines, e, 1) for e in (2, 1, 3)}
    pieces = [lines, came[1], came[2], came[3]]

    pairs = solved0.reshape(2 * K // 4, 2 * TB)
    mine, theirs = pairs[:, :TB], partner(pairs[:, TB:])
    mine, theirs = mine.reshape(16, 16, TB), theirs.reshape(16, 16, TB)
    own0 = jnp.where(
        core == 0, jnp.stack([mine, theirs], 1), jnp.stack([theirs, mine], 1)
    ).reshape(K, TB)
    came = [own0] + [shifted(own0, "x", d, SHIFTS) for d in (1, 2, 3)]
    [pair] = local(functools.partial(pick, 0), [((2, K, TB), BF16)], *came)
    all0 = [pair] + [shifted(pair, "y", e, SHIFTS) for e in (1, 2, 3)]

    early, tiles = local(
        early_part, [((2, TB, K), F32), ((CHIPS, 2, TB, TB), BF16)], *tiles, *all0,
        flops=2**28,
    )
    theirs, solved1 = local(
        part_of_partner, [((TB, K), F32), ((CHIPS, ROWS, 32, TB), BF16)], tiles, *pieces, early,
        flops=2**27,
    )
    theirs = partner(theirs)
    left, solved = local(
        own_part, [((TB, K), F32), ((TB, K), BF16)], tiles, solved1, early, own0,
        rhs_trail.reshape(TB, K), flops=2**27,
    )
    remaining = (left - theirs).astype(BF16)
    return solved.reshape(1, 1, TB, K), remaining.reshape(rhs_trail.shape)


def solution(mesh):
    torus = Mesh(mesh.devices.reshape(mesh.shape["row"], 4, 4, 2), ("row", *COL))
    placed = (
        P(None, None, "row", None, None),
        P(None, None, "row", None, None, COL, None),
        P(None, None, "row", None, COL),
        P(None, COL, None, None),
        P(None, "row", None, None, COL, None),
        P(None, "row", None, COL),
        P(COL, None, "row", None, None),
    )
    return jax.shard_map(
        steps,
        mesh=torus,
        in_specs=placed,
        out_specs=(P(None, COL, None, None), P(COL, None, "row", None, None)),
        check_vma=False,
    )
```

```python
import functools
import math

import jax
import jax.numpy as jnp
from jax import lax
from jax.experimental import pallas as pl
from jax.experimental.pallas import tpu as pltpu
from jax.sharding import Mesh
from jax.sharding import PartitionSpec as P


TB = 128
COL = ("x", "y", "core")
CHIP = ("x", "y")
ROWS = 8
CHIPS = 16
K = 512
F32 = jnp.float32
BF16 = jnp.bfloat16
SHIFTS = (0, 1, 2, 3)


def exchange(x, axis):
    return lax.all_to_all(x, axis, split_axis=0, concat_axis=0, tiled=True)


def partner(x):
    return lax.ppermute(x, "core", [(0, 1), (1, 0)])


def shifted(x, axis, step, sources):
    return lax.ppermute(x, axis, [(i, (i + step) % 4) for i in sources])


def crossed_groups():
    groups = []
    for core in range(2):
        for other in range(4):
            group = []
            for along in range(4):
                x, y = (along, other) if core == 0 else (other, along)
                group += [r * 32 + x * 8 + y * 2 + core for r in range(ROWS)]
            groups.append(group)
    return groups


def crossed(x, step, phase):
    pairs = []
    for i in range(32):
        at = [i // 8, i // 2 % 4, i % 2]
        at[(i + phase) % 2] = (at[(i + phase) % 2] + step) % 4
        pairs.append((i, at[0] * 8 + at[1] * 2 + at[2]))
    return lax.ppermute(x, COL, pairs)


def crossed_here():
    first = lax.axis_index("core") == 0
    x, y = here()
    return jnp.where(first, x, y), jnp.where(first, y, x), first


def dot_nt(a, b):
    return lax.dot_general(a, b, (((1,), (1,)), ((), ())), preferred_element_type=F32)


def here():
    return lax.axis_index("x"), lax.axis_index("y")


def back(index, step):
    return lax.rem(index - step + 4, 4)


def local(kernel, outs, *args, smem=(), flops=1_000_000):
    size = sum(a.size * a.dtype.itemsize for a in args)
    kept = size + sum(math.prod(shape) * jnp.dtype(dtype).itemsize for shape, dtype in outs)
    specs = [
        pl.BlockSpec(memory_space=pltpu.SMEM if i in smem else pltpu.VMEM)
        for i in range(len(args))
    ]
    return pl.pallas_call(
        kernel,
        out_shape=[jax.ShapeDtypeStruct(shape, dtype) for shape, dtype in outs],
        in_specs=specs,
        out_specs=[pl.BlockSpec(memory_space=pltpu.VMEM) for _ in outs],
        cost_estimate=pl.CostEstimate(flops=flops, bytes_accessed=2 * size, transcendentals=0),
        compiler_params=pltpu.CompilerParams(vmem_limit_bytes=kept + 2**21),
    )(*args)


def turned(given, out):
    lines = jnp.concatenate([given[0].T, given[1].T], axis=1)
    lines = lines.reshape(16, 2, 16, 2 * TB)
    lines = jnp.where(lax.axis_index("core") == 0, lines[:, 0], lines[:, 1])
    out[...] = lines.reshape(ROWS, 32, 2 * TB)


def send_first(factor, mask, *outs):
    u, _, first = crossed_here()
    far, near = jnp.where(first, 8, 2), jnp.where(first, 2, 8)
    for d, out in enumerate(outs):
        base = lax.rem(u + d, 4) * far
        for v in range(4):
            for kk in range(2):
                t = base + v * near + kk
                out[2 * v + kk] = jnp.where(mask[t] == 1, factor[t], jnp.zeros((TB, TB), BF16))


def send_second(*refs):
    came, outs = refs[:4], refs[4:]
    _, v, _ = crossed_here()
    for e, out in enumerate(outs):
        base = lax.rem(v + e, 4) * 2
        for d in SHIFTS:
            out[2 * d] = came[d][base]
            out[2 * d + 1] = came[d][base + 1]


def pick(first, *refs):
    came, out = refs[:4], refs[4]
    x, _ = here()
    for d in SHIFTS:
        side = back(x, d) - first

        @pl.when(jnp.logical_and(side >= 0, side < 2))
        def _(d=d, side=side):
            out[side] = came[d][...]


def first_rows(due, own, other, out):
    lines = jnp.concatenate(
        [due[r][:, a * TB : (a + 1) * TB] for a in range(2) for r in range(ROWS)], axis=1
    )
    both = jnp.concatenate([dot_nt(lines, own[...]), dot_nt(lines, other[...])], axis=1)
    both = both.astype(BF16)
    for r in range(ROWS):
        out[r] = both


def update(solved, own, other, out):
    tiles = jnp.concatenate([own[...], other[...]], axis=1)
    reached = dot_nt(solved[...].reshape(256, 256), tiles)
    out[...] = reached.reshape(CHIPS, 16, 2 * TB)


def due_rows(came, given, out):
    reached = came[0]
    for chip in range(1, 8):
        reached = reached + came[chip]
    out[...] = (given[...].astype(F32) - reached).astype(BF16)


def second_rows(mine, theirs, *refs):
    pieces, out = refs[:4], refs[4]
    _, y = here()
    first = lax.axis_index("core") == 0
    a, b = mine[...], theirs[...]
    due = jnp.concatenate([jnp.where(first, a, b), jnp.where(first, b, a)], axis=0)
    for e in SHIFTS:
        for side in range(2):
            out[side * 4 + back(y, e)] = dot_nt(due, pieces[e][side])


def second_sum(came, out):
    total = came[0]
    for r in range(1, ROWS):
        total = total + came[r]
    total = total.astype(BF16)
    for place in range(4 * ROWS):
        out[place] = total


def early_part(*refs):
    came, solved, out, tiles = refs[:4], refs[4:8], *refs[8:]
    _, y = here()
    u, v, first = crossed_here()
    for e in SHIFTS:
        for d in SHIFTS:
            at_u, at_v = back(u, d), back(v, e)
            tiles[jnp.where(first, at_u * 4 + at_v, at_v * 4 + at_u)] = came[e][2 * d : 2 * d + 2]
    total = jnp.zeros((2 * TB, K), F32)
    for e in SHIFTS:
        for side in range(2):
            block = tiles[side * 4 + back(y, e)].reshape(2 * TB, TB)
            total = total + dot_nt(block, solved[e][side])
    out[...] = total.reshape(2, TB, K)


def late_part(tiles, solved, which):
    total = jnp.zeros((TB, K), F32)
    for tile in range(8):
        total = total + dot_nt(tiles[8 + tile, which], solved[:, tile].reshape(K, TB))
    return total


def part_of_partner(*refs):
    tiles, pieces, early, out, solved = refs[0], refs[1:5], *refs[5:]
    _, v, first = crossed_here()
    for e in SHIFTS:
        source = back(v, e)
        for u in range(4):
            solved[jnp.where(first, u * 4 + source, source * 4 + u)] = pieces[e][u]
    which = 1 - lax.axis_index("core")
    out[...] = early[which] + late_part(tiles, solved, which)


def own_part(tiles, solved, early, solved0, given, left, result):
    which = lax.axis_index("core")
    left[...] = given[...].astype(F32) - (early[which] + late_part(tiles, solved, which))
    chip = lax.axis_index("x") * 4 + lax.axis_index("y")

    @pl.when(chip < 8)
    def _():
        result[...] = solved0[...].T

    @pl.when(chip >= 8)
    def _():
        result[...] = solved[:, chip - 8].reshape(K, TB).T


def steps(rhs_super, factor_super, mask_super, dinv_rows, factor_trail, mask_trail, rhs_trail):
    core = lax.axis_index("core")
    chip = lax.axis_index(CHIP)

    [rhs0] = local(turned, [((ROWS, 32, 2 * TB), BF16)], rhs_super[0].reshape(2, TB, K))
    rhs0, dinv, factor_trail, rhs_super = lax.optimization_barrier(
        (rhs0, dinv_rows[0, 0], factor_trail, rhs_super)
    )
    due0 = exchange(rhs0, "row")
    dinv_other = partner(dinv)
    row = lax.axis_index("row")
    d1 = jnp.concatenate(
        [lax.dynamic_slice(dinv, (0, (a * ROWS + row) * TB), (TB, TB)) for a in range(2)], 1
    )
    came = [d1] + [shifted(d1, "x", d, SHIFTS) for d in (1, 2, 3)]
    [d1] = local(functools.partial(pick, 2), [((2, TB, 2 * TB), BF16)], *came)
    d1 = [d1] + [shifted(d1, "y", e, SHIFTS) for e in (1, 2, 3)]

    mask = mask_trail.reshape(32)
    sent = local(
        send_first, [((8, TB, TB), BF16)] * 4, factor_trail.reshape(32, TB, TB), mask,
        smem=(1,),
    )
    came = [sent[0]] + [crossed(sent[d], d, 0) for d in (1, 2, 3)]
    sent = local(send_second, [((8, TB, TB), BF16)] * 4, *came)
    tiles = [sent[0]] + [crossed(sent[e], e, 1) for e in (1, 2, 3)]

    [solved0] = local(
        first_rows, [((ROWS, 32, 2 * TB), BF16)], due0, dinv, dinv_other,
        flops=2**26,
    )
    solved0 = exchange(solved0, "row")

    keep = mask_super[1].astype(BF16).reshape(2, 1, 1)
    tiles10 = (factor_super[1].reshape(2, TB, TB) * keep).reshape(2 * TB, TB)
    [reached] = local(
        update, [((CHIPS, 16, 2 * TB), F32)], solved0, tiles10, partner(tiles10),
        flops=2**25,
    )
    reached = exchange(reached, CHIP)
    rhs1 = rhs_super[1, :, 0].reshape(2 * TB, K)
    rhs1 = lax.dynamic_slice(rhs1, (0, chip * 32 + core * 16), (2 * TB, 16)).T
    [due1] = local(due_rows, [((16, 2 * TB), BF16)], reached, rhs1)
    [part] = local(
        second_rows, [((ROWS, 32, TB), F32)], due1, partner(due1), *d1,
        flops=2**25,
    )
    part = exchange(part, "row")
    [solved1] = local(second_sum, [((4 * ROWS, 32, TB), BF16)], part)
    lines = lax.all_to_all(
        solved1, ("row", *COL), 0, 0, axis_index_groups=crossed_groups(), tiled=True
    ).reshape(4, ROWS, 32, TB)
    came = {e: crossed(lines, e, 1) for e in (2, 1, 3)}
    pieces = [lines, came[1], came[2], came[3]]

    pairs = solved0.reshape(2 * K // 4, 2 * TB)
    mine, theirs = pairs[:, :TB], partner(pairs[:, TB:])
    mine, theirs = mine.reshape(16, 16, TB), theirs.reshape(16, 16, TB)
    own0 = jnp.where(
        core == 0, jnp.stack([mine, theirs], 1), jnp.stack([theirs, mine], 1)
    ).reshape(K, TB)
    came = [own0] + [shifted(own0, "x", d, SHIFTS) for d in (1, 2, 3)]
    [pair] = local(functools.partial(pick, 0), [((2, K, TB), BF16)], *came)
    all0 = [pair] + [shifted(pair, "y", e, SHIFTS) for e in (1, 2, 3)]

    early, tiles = local(
        early_part, [((2, TB, K), F32), ((CHIPS, 2, TB, TB), BF16)], *tiles, *all0,
        flops=2**28,
    )
    theirs, solved1 = local(
        part_of_partner, [((TB, K), F32), ((CHIPS, ROWS, 32, TB), BF16)], tiles, *pieces, early,
        flops=2**27,
    )
    theirs = partner(theirs)
    left, solved = local(
        own_part, [((TB, K), F32), ((TB, K), BF16)], tiles, solved1, early, own0,
        rhs_trail.reshape(TB, K), flops=2**27,
    )
    remaining = (left - theirs).astype(BF16)
    return solved.reshape(1, 1, TB, K), remaining.reshape(rhs_trail.shape)


def solution(mesh):
    torus = Mesh(mesh.devices.reshape(mesh.shape["row"], 4, 4, 2), ("row", *COL))
    placed = (
        P(None, None, "row", None, None),
        P(None, None, "row", None, None, COL, None),
        P(None, None, "row", None, COL),
        P(None, COL, None, None),
        P(None, "row", None, None, COL, None),
        P(None, "row", None, COL),
        P(COL, None, "row", None, None),
    )
    return jax.shard_map(
        steps,
        mesh=torus,
        in_specs=placed,
        out_specs=(P(None, COL, None, None), P(COL, None, "row", None, None)),
        check_vma=False,
    )
```
